32 devices in a mesh: dp: 4 (over z), blk: 4 (over x, core), head: 2 (over y).
Axes of the slice: x: 2, y: 2, z: 4, core: 2. Of those that a mesh axis runs over, the one named last changes fastest.
Arguments:
- tokens: bfloat16 [16384, 2048], P(('dp', 'blk', 'head')), may hold values from -6 to 6
- cotangent: bfloat16 [16384, 2048], P(('dp', 'blk', 'head')), may hold values from -6 to 6
- segment: int32 [16384], P(('dp', 'blk', 'head')), may hold values from 0 to 8, as said below
- position: int32 [16384], P(('dp', 'blk', 'head')), may hold values from 0 to 2303, as said below
- ln1_gain: float32 [2048], replicated, may hold values from 0.5 to 1.5
- ln1_bias: float32 [2048], replicated, may hold values from -3 to 3
- ln2_gain: float32 [2048], replicated, may hold values from 0.5 to 1.5
- ln2_bias: float32 [2048], replicated, may hold values from -3 to 3
- w_qkv: bfloat16 [2048, 6144], P(('dp', 'blk', 'head')), may hold values from -0.125 to 0.125
- b_qkv: float32 [6144], replicated, may hold values from -3 to 3
- w_out: bfloat16 [2048, 2048], P(('dp', 'blk', 'head')), may hold values from -0.5 to 0.5
- b_out: float32 [2048], replicated, may hold values from -3 to 3
- w_up: bfloat16 [2048, 8192], P(('dp', 'blk', 'head')), may hold values from -0.125 to 0.125
- b_up: float32 [8192], replicated, may hold values from -3 to 3
- w_down: bfloat16 [2048, 8192], P(('dp', 'blk', 'head')), may hold values from -0.0625 to 0.0625
- b_down: float32 [2048], replicated, may hold values from -3 to 3
Outputs:
- block_output: bfloat16 [16384, 2048], P(('dp', 'blk', 'head'))
- d_tokens: float32 [16384, 2048], P(('dp', 'blk', 'head'))
- grad_ln1_gain: float32 [2048], replicated
- grad_ln1_bias: float32 [2048], replicated
- grad_ln2_gain: float32 [2048], replicated
- grad_ln2_bias: float32 [2048], replicated
- grad_w_qkv: float32 [2048, 6144], P(('dp', 'blk', 'head'))
- grad_b_qkv: float32 [6144], replicated
- grad_w_out: float32 [2048, 2048], P(('dp', 'blk', 'head'))
- grad_b_out: float32 [2048], replicated
- grad_w_up: float32 [2048, 8192], P(('dp', 'blk', 'head'))
- grad_b_up: float32 [8192], replicated
- grad_w_down: float32 [2048, 8192], P(('dp', 'blk', 'head'))
- grad_b_down: float32 [2048], replicated
The draws below stay inside these ranges and needn't reach their ends.
Inputs may be any that keep to these rules, and one draw needn't show every extreme that they name: Rows form groups of 4096 starting at multiples of 4096, each made of aligned runs of 256 rows of one segment. In a group, segment 0 holds 2048 rows and each of segments 1 to 8 holds 256 rows; the runs stand in any order. `position`: within a run of 256 rows positions rise by one. In a group, the prompt rows carry each of 0 to 2047 once, and every continuation carries 2048 to 2303 in order.
All inputs are finite; a program needn't handle non-finite values.
Results may differ from the reference program's by a relative error of at most 0.0096.
Values may be sent and summed in bfloat16 or wider, within the bound.
No kernel may reach another device: no remote copies, remote signals or barrier semaphores. Data moves between devices by JAX's collectives and lax.ppermute only.
A program may use at most 512 MiB of HBM per device.

```python
import math
import jax
import jax.numpy as jnp
from jax import lax

D = 2048
HEADS = 8
HD = 256
ROT = 64
FF = 8192
PROMPT = 2048
CONT = 256
GROUP_TOK = 4096
TOKENS = 16384


def layout_ids(key):
    block_total = GROUP_TOK // CONT
    prompt_blocks = PROMPT // CONT
    group_total = TOKENS // GROUP_TOK
    group_keys = jax.random.split(jax.random.fold_in(key, 7), group_total)

    def one_group(group_key):
        order = jax.random.permutation(group_key, block_total).astype(jnp.int32)
        within = jnp.arange(CONT, dtype=jnp.int32)
        is_prompt = order < prompt_blocks
        seg_block = jnp.where(is_prompt, 0, order - prompt_blocks + 1).astype(jnp.int32)
        start_pos = jnp.where(is_prompt, order * CONT, PROMPT).astype(jnp.int32)
        seg_rows = (seg_block[:, None] + jnp.zeros((1, CONT), jnp.int32)).reshape(-1)
        pos_rows = (start_pos[:, None] + within[None, :]).reshape(-1)
        return (seg_rows, pos_rows)
    seg_all, pos_all = jax.vmap(one_group)(group_keys)
    return (seg_all.reshape(-1).astype(jnp.int32), pos_all.reshape(-1).astype(jnp.int32))


def draw_segment(key, part):
    return layout_ids(key)[0]


def draw_position(key, part):
    return layout_ids(key)[1]


def spiked(array, rng, source, target, blocks, factor):
    owner, partner = [(jnp.arange(array.shape[axis_at]) // (array.shape[axis_at] // blocks)).reshape([-1 if axis == axis_at else 1 for axis in range(array.ndim)]) for axis_at in (source, target)]
    chosen = jax.random.permutation(rng, blocks)[partner]
    strong = (owner == chosen) | (owner == (partner + blocks // 2) % blocks)
    return jnp.where(strong, factor * array, array)


def steps_of(stream_key, shape, pieces, low, largest):
    loudness, own = 1.0, jax.random.fold_in(stream_key, 6)
    for dim, blocks in pieces:
        steps = jnp.exp(jax.random.uniform(jax.random.fold_in(own, dim), (blocks,), jnp.float32, low / len(pieces), largest / len(pieces)))
        loudness = loudness * jnp.repeat(steps, shape[dim] // blocks).reshape([-1 if axis == dim else 1 for axis in range(len(shape))])
    return loudness


def gaussian(rng, dims, width, limit, cuts=(), kind=jnp.bfloat16):
    drawn = jax.random.normal(rng, dims, jnp.float32) * width
    if len(cuts) > 0:
        drawn = steps_of(rng, dims, cuts, -0.22, 0.18) * drawn
    return jnp.clip(drawn, min=-limit, max=limit).astype(kind)


def gaussian_with(own_key, shape, width, most, cuts, heavy, kind=jnp.bfloat16):
    values = width * jax.random.normal(own_key, shape, jnp.float32)
    if cuts:
        values = values * steps_of(own_key, shape, cuts, -0.22, 0.18)
    return jnp.clip(spiked(values, jax.random.fold_in(own_key, 3), *heavy), -most, most).astype(kind)


def setup_inputs(seed: int = 0) -> dict:
    keys = jax.random.split(jax.random.key(seed), 17)
    return {
        "tokens": gaussian(keys[0], (TOKENS, D), 1.0, 6.0, ((0, 32),)),
        "cotangent": gaussian_with(keys[1], (TOKENS, D), 1.0, 6.0, ((0, 32),), (0, 1, 32, 2.75)),
        "segment": draw_segment(jax.random.fold_in(keys[16], 71), 0),
        "position": draw_position(jax.random.fold_in(keys[16], 71), 0),
        "ln1_gain": jnp.clip(1.0 + 0.1 * jax.random.normal(keys[4], (D,), jnp.float32), 0.5, 1.5),
        "ln1_bias": gaussian(keys[5], (D,), 0.5, 3.0, (), jnp.float32),
        "ln2_gain": jnp.clip(1.0 + 0.1 * jax.random.normal(keys[6], (D,), jnp.float32), 0.5, 1.5),
        "ln2_bias": gaussian(keys[7], (D,), 0.5, 3.0, (), jnp.float32),
        "w_qkv": gaussian(keys[8], (D, 3 * D), D ** -0.5, 0.125, ((0, 32),)),
        "b_qkv": gaussian(keys[9], (3 * D,), 0.5, 3.0, (), jnp.float32),
        "w_out": gaussian(keys[10], (D, D), (D // 16) ** -0.5, 0.5, ((0, 32),)),
        "b_out": gaussian(keys[11], (D,), 0.5, 3.0, (), jnp.float32),
        "w_up": gaussian(keys[12], (D, FF), D ** -0.5, 0.125, ((0, 32),)),
        "b_up": gaussian(keys[13], (FF,), 0.5, 3.0, (), jnp.float32),
        "w_down": gaussian(keys[14], (D, FF), FF ** -0.5, 0.0625, ((0, 32),)),
        "b_down": gaussian(keys[15], (D,), 0.5, 3.0, (), jnp.float32),
    }


@jax.custom_vjp
def low(v):
    return lax.optimization_barrier(v.astype(jnp.bfloat16)).astype(jnp.float32)

@jax.custom_vjp
def low_back(v):
    return v

def low_keep(v):
    return (low(v), None)

def low_pass(kept, grad):
    return (grad,)

def back_keep(v):
    return (v, None)

def back_low(kept, grad):
    return (low(grad),)
low.defvjp(low_keep, low_pass)
low_back.defvjp(back_keep, back_low)
highest = lax.Precision.HIGHEST

def layer_norm(values, norm_gain, norm_bias):
    average = lax.optimization_barrier(jnp.mean(values, axis=-1, keepdims=True))
    centered = values - average
    variance = lax.optimization_barrier(jnp.mean(centered * centered, axis=-1, keepdims=True))
    return centered * lax.rsqrt(variance + 1e-05) * norm_gain + norm_bias

def rotate(tensor, positions):
    half_dims = ROT // 2
    frequency = jnp.exp(jnp.arange(half_dims, dtype=jnp.float32) * (-2.0 * math.log(10000.0) / ROT))
    angles = positions.astype(jnp.float32)[:, None] * frequency[None, :]
    cosine = jnp.cos(angles)[:, None, :]
    sine_val = jnp.sin(angles)[:, None, :]
    first_half = tensor[..., :half_dims]
    second_half = tensor[..., half_dims:ROT]
    untouched = tensor[..., ROT:]
    return jnp.concatenate([first_half * cosine - second_half * sine_val, second_half * cosine + first_half * sine_val, untouched], axis=-1)

def visible(seg_q, pos_q, seg_k, pos_k):
    same_seg = seg_q[:, None] == seg_k[None, :]
    causal = pos_k[None, :] <= pos_q[:, None]
    prompt_key = (seg_k[None, :] == 0) & (seg_q[:, None] != 0)
    return same_seg & causal | prompt_key

def forward_group(block_in, seg_ids, positions, params):
    ln1_g, ln1_b, ln2_g, ln2_b, w_qkv, b_qkv, w_out, b_out, w_up, b_up, w_down, b_down = params
    row_total = block_in.shape[0]
    attn_input = low(layer_norm(block_in, ln1_g, ln1_b))
    qkv_linear = low_back(jnp.dot(attn_input, w_qkv, precision=highest) + b_qkv)
    qkv_split = qkv_linear.reshape(row_total, 3, HEADS, HD)
    queries = low_back(low(rotate(qkv_split[:, 0], positions)))
    keys_rot = low_back(low(rotate(qkv_split[:, 1], positions)))
    values_all = low_back(low(qkv_split[:, 2]))
    block_rows = math.gcd(row_total, 512)
    score_scale = HD ** (-0.5)

    def attend(inputs):
        query_blk, seg_blk, pos_blk = inputs
        scores = jnp.einsum('qhd,khd->hqk', query_blk, keys_rot, precision=highest) * score_scale
        scores = low_back(scores)
        visible_mask = visible(seg_blk, pos_blk, seg_ids, positions)[None]
        scores = jnp.where(visible_mask, scores, -1e+30)
        row_max = lax.optimization_barrier(jnp.max(scores, axis=-1, keepdims=True))
        unnormed = jnp.exp(scores - row_max)
        prob_low = low(unnormed / lax.optimization_barrier(jnp.sum(unnormed, axis=-1, keepdims=True)))
        return jnp.einsum('hqk,khd->qhd', prob_low, values_all, precision=highest)
    block_count = row_total // block_rows
    attended = lax.map(jax.checkpoint(attend), (queries.reshape(block_count, block_rows, HEADS, HD), seg_ids.reshape(block_count, block_rows), positions.reshape(block_count, block_rows)))
    attn = low_back(low(attended.reshape(row_total, D)))
    attn_branch = jnp.dot(attn, w_out, precision=highest) + b_out
    mlp_input = low(layer_norm(block_in, ln2_g, ln2_b))
    up_linear = low_back(jnp.dot(mlp_input, w_up, precision=highest) + b_up)
    activation = low(jax.nn.gelu(up_linear, approximate=False))
    mlp_branch = jnp.dot(activation, w_down.T, precision=highest) + b_down
    return block_in + attn_branch + mlp_branch

def reference(tokens, cotangent, segment, position, ln1_gain, ln1_bias, ln2_gain, ln2_bias, w_qkv, b_qkv, w_out, b_out, w_up, b_up, w_down, b_down):
    params = tuple((p.astype(jnp.float32) for p in (ln1_gain, ln1_bias, ln2_gain, ln2_bias, w_qkv, b_qkv, w_out, b_out, w_up, b_up, w_down, b_down)))
    group_total = tokens.shape[0] // GROUP_TOK
    inputs_f32 = tokens.astype(jnp.float32).reshape(group_total, GROUP_TOK, D)
    cot_f32 = cotangent.astype(jnp.float32).reshape(group_total, GROUP_TOK, D)
    seg_groups = segment.reshape(group_total, GROUP_TOK)
    pos_groups = position.reshape(group_total, GROUP_TOK)
    zero_grads = jax.tree.map(jnp.zeros_like, params)

    def group_step(grad_sum, group_item):
        block_in, block_cot, seg_ids, positions = group_item
        group_out, pullback = jax.vjp(lambda inner_x, inner_p: forward_group(inner_x, seg_ids, positions, inner_p), block_in, params)
        d_input, d_params = pullback(block_cot)
        return (jax.tree.map(jnp.add, grad_sum, d_params), (group_out, d_input))
    grads, (group_outs, d_inputs) = lax.scan(group_step, zero_grads, (inputs_f32, cot_f32, seg_groups, pos_groups))
    return (group_outs.reshape(-1, D).astype(jnp.bfloat16), d_inputs.reshape(-1, D), grads[0], grads[1], grads[2], grads[3], grads[4], grads[5], grads[6], grads[7], grads[8], grads[9], grads[10], grads[11])
```

```python
from functools import partial
import math

import jax
import jax.numpy as jnp
from jax import lax
from jax.experimental import pallas as pl
from jax.experimental.pallas import tpu as pltpu
from jax.sharding import PartitionSpec as P

HEADS = 8
HD = 256
ROT = 64


def layer_norm(values, norm_gain, norm_bias):
    average = jnp.mean(values, axis=-1, keepdims=True)
    centered = values - average
    variance = jnp.mean(centered * centered, axis=-1, keepdims=True)
    return centered * lax.rsqrt(variance + 1e-05) * norm_gain + norm_bias


def rotate(tensor, positions):
    half_dims = ROT // 2
    frequency = jnp.exp(jnp.arange(half_dims, dtype=jnp.float32) * (-2.0 * math.log(10000.0) / ROT))
    angles = positions.astype(jnp.float32)[:, None] * frequency[None, :]
    cosine = jnp.cos(angles)[:, None, :]
    sine_val = jnp.sin(angles)[:, None, :]
    first_half = tensor[..., :half_dims]
    second_half = tensor[..., half_dims:ROT]
    untouched = tensor[..., ROT:]
    return jnp.concatenate(
        [
            first_half * cosine - second_half * sine_val,
            second_half * cosine + first_half * sine_val,
            untouched,
        ],
        axis=-1,
    )


def rotate_parts(linear, positions):
    return jnp.stack(
        [rotate(linear[:, 0], positions), rotate(linear[:, 1], positions), linear[:, 2]], axis=1
    )


def visible(seg_q, pos_q, seg_k, pos_k):
    same_seg = seg_q[:, None] == seg_k[None, :]
    causal = pos_k[None, :] <= pos_q[:, None]
    prompt_key = (seg_k[None, :] == 0) & (seg_q[:, None] != 0)
    return same_seg & causal | prompt_key


def shards_by_blocks(
    tokens,
    cotangent,
    segment,
    position,
    ln1_gain,
    ln1_bias,
    ln2_gain,
    ln2_bias,
    w_qkv,
    b_qkv,
    w_out,
    b_out,
    w_up,
    b_up,
    w_down,
    b_down,
):
    tok_rows = tokens.shape[0]
    model_width = tokens.shape[1]
    hidden_units = w_up.shape[1]
    head_dim = HD
    head_count = lax.axis_size("head")
    local_heads = HEADS // head_count
    col_width = model_width // head_count
    ff_cols = hidden_units // head_count
    head_index = lax.axis_index("head")
    weight_owners = lax.axis_size("dp") * lax.axis_size("blk")
    owner_rows = w_qkv.shape[0]
    contract_last = (((1,), (1,)), ((), ()))
    contract_rows = (((0,), (0,)), ((), ()))
    row_seg, row_pos = (
        lax.all_gather(segment, ("blk", "head"), axis=0, tiled=True),
        lax.all_gather(position, ("blk", "head"), axis=0, tiled=True),
    )
    shard_rows = tok_rows * head_count
    first_row = lax.axis_index("blk") * shard_rows
    seg_local = lax.dynamic_slice_in_dim(row_seg, first_row, shard_rows)
    pos_local = lax.dynamic_slice_in_dim(row_pos, first_row, shard_rows)
    tokens_f32 = tokens.astype(jnp.float32)
    cot_f32 = cotangent.astype(jnp.float32)
    normed_one, norm_back_one = jax.vjp(layer_norm, tokens_f32, ln1_gain, ln1_bias)
    attn_input = normed_one.astype(jnp.bfloat16)
    normed_two, norm_back_two = jax.vjp(layer_norm, tokens_f32, ln2_gain, ln2_bias)
    mlp_input = normed_two.astype(jnp.bfloat16)
    qkv_parts = w_qkv.reshape(owner_rows, 3, head_count, col_width)
    out_parts = w_out.reshape(owner_rows, 1, head_count, col_width)
    up_parts = w_up.reshape(owner_rows, 1, head_count, ff_cols)
    down_parts = w_down.reshape(owner_rows, 1, head_count, ff_cols)
    slice_qkv, slice_out, slice_up, slice_down = (
        lax.all_to_all(qkv_parts, "head", split_axis=2, concat_axis=0, tiled=True),
        lax.all_to_all(out_parts, "head", split_axis=2, concat_axis=0, tiled=True),
        lax.all_to_all(up_parts, "head", split_axis=2, concat_axis=0, tiled=True),
        lax.all_to_all(down_parts, "head", split_axis=2, concat_axis=0, tiled=True),
    )
    whole_qkv, whole_out, whole_up, whole_down = (
        lax.all_gather(slice_qkv, ("dp", "blk"), axis=0, tiled=True),
        lax.all_gather(slice_out, ("dp", "blk"), axis=0, tiled=True),
        lax.all_gather(slice_up, ("dp", "blk"), axis=0, tiled=True),
        lax.all_gather(slice_down, ("dp", "blk"), axis=0, tiled=True),
    )
    qkv_cols = whole_qkv.reshape(model_width, 3 * col_width)
    out_cols = whole_out.reshape(model_width, col_width)
    up_cols = whole_up.reshape(model_width, ff_cols)
    down_cols = whole_down.reshape(model_width, ff_cols)
    attn_rows, mlp_rows, cot_rows = (
        lax.all_gather(attn_input, "head", axis=0, tiled=True),
        lax.all_gather(mlp_input, "head", axis=0, tiled=True),
        lax.all_gather(cotangent, "head", axis=0, tiled=True),
    )
    bias_local = lax.dynamic_index_in_dim(
        b_qkv.reshape(3, head_count, col_width), head_index, 1, keepdims=False
    ).reshape(3 * col_width)
    qkv_linear = jnp.dot(attn_rows, qkv_cols, preferred_element_type=jnp.float32) + bias_local
    qkv_split = qkv_linear.reshape(shard_rows, 3, local_heads, head_dim)
    rotated, rotary_back = jax.vjp(lambda linear: rotate_parts(linear, pos_local), qkv_split)
    by_head = rotated.astype(jnp.bfloat16)
    queries = by_head[:, 0]
    keys_vals = lax.all_gather(by_head[:, 1:], "blk", axis=0, tiled=True)
    keys_all = keys_vals[:, 0]
    values_all = keys_vals[:, 1]
    group_rows = keys_all.shape[0]
    score_rows = math.gcd(shard_rows, 512)
    block_count = shard_rows // score_rows
    score_scale = head_dim ** (-0.5)
    query_blocks = queries.reshape(block_count, score_rows, local_heads, head_dim)
    seg_blocks = seg_local.reshape(block_count, score_rows)
    pos_blocks = pos_local.reshape(block_count, score_rows)

    def scores_of(query_blk, seg_blk, pos_blk):
        raw_scores = (
            jnp.einsum("qhd,khd->hqk", query_blk, keys_all, preferred_element_type=jnp.float32)
            * score_scale
        )
        visible_mask = visible(seg_blk, pos_blk, row_seg, row_pos)[None]
        return jnp.where(visible_mask, raw_scores, -1e30)

    def forward_block(inputs):
        query_blk, seg_blk, pos_blk = inputs
        scores = scores_of(query_blk, seg_blk, pos_blk)
        row_max = jnp.max(scores, axis=-1, keepdims=True)
        unnormed = jnp.exp(scores - row_max)
        row_sum = jnp.sum(unnormed, axis=-1, keepdims=True)
        prob_bf16 = (unnormed / row_sum).astype(jnp.bfloat16)
        attended = jnp.einsum(
            "hqk,khd->qhd", prob_bf16, values_all, preferred_element_type=jnp.float32
        )
        return (attended, (row_max + jnp.log(row_sum))[..., 0])

    attended_all, log_total = lax.map(forward_block, (query_blocks, seg_blocks, pos_blocks))
    attn_heads = attended_all.reshape(shard_rows, local_heads, head_dim).astype(jnp.bfloat16)
    attn_full = lax.all_gather(
        attn_heads.reshape(shard_rows, col_width), "head", axis=1, tiled=True
    )
    out_bias = lax.dynamic_slice_in_dim(b_out, head_index * col_width, col_width)
    branch_cols = jnp.dot(attn_full, out_cols, preferred_element_type=jnp.float32) + out_bias
    attn_branch = lax.all_to_all(branch_cols, "head", split_axis=0, concat_axis=1, tiled=True)
    up_bias = lax.dynamic_slice_in_dim(b_up, head_index * ff_cols, ff_cols)
    up_linear = jnp.dot(mlp_rows, up_cols, preferred_element_type=jnp.float32) + up_bias
    activation, gelu_back = jax.vjp(partial(jax.nn.gelu, approximate=False), up_linear)
    act_bf16 = activation.astype(jnp.bfloat16)
    mlp_terms = lax.dot_general(
        act_bf16, down_cols, contract_last, preferred_element_type=jnp.float32
    )
    mlp_branch = lax.psum_scatter(
        mlp_terms.astype(jnp.bfloat16), "head", scatter_dimension=0, tiled=True
    ).astype(jnp.float32)
    block_output = (tokens_f32 + attn_branch + mlp_branch + b_down).astype(jnp.bfloat16)
    d_act = jnp.dot(cot_rows, down_cols, preferred_element_type=jnp.float32)
    d_up_bf16 = gelu_back(d_act)[0].astype(jnp.bfloat16)
    d_two_terms = lax.dot_general(
        d_up_bf16, up_cols, contract_last, preferred_element_type=jnp.float32
    )
    cot_cols = lax.dynamic_slice_in_dim(cot_rows, head_index * col_width, col_width, 1)
    d_attn_terms = lax.dot_general(
        cot_cols, out_cols, contract_last, preferred_element_type=jnp.float32
    )
    d_attn_sum = lax.psum_scatter(d_attn_terms, "head", scatter_dimension=1, tiled=True)
    d_heads = d_attn_sum.astype(jnp.bfloat16).reshape(shard_rows, local_heads, head_dim)
    d_blocks = d_heads.reshape(block_count, score_rows, local_heads, head_dim)

    def backward_block(carried, inputs):
        d_key, d_value = carried
        query_blk, seg_blk, pos_blk, total_blk, d_out = inputs
        scores = scores_of(query_blk, seg_blk, pos_blk)
        prob_f32 = jnp.exp(scores - total_blk[..., None])
        prob_bf16 = prob_f32.astype(jnp.bfloat16)
        d_probs = jnp.einsum("qhd,khd->hqk", d_out, values_all, preferred_element_type=jnp.float32)
        inner_sum = jnp.sum(prob_f32 * d_probs, axis=-1, keepdims=True)
        d_scores = (prob_f32 * (d_probs - inner_sum)).astype(jnp.bfloat16)
        d_query = (
            jnp.einsum("hqk,khd->qhd", d_scores, keys_all, preferred_element_type=jnp.float32)
            * score_scale
        )
        d_key = (
            d_key
            + jnp.einsum("hqk,qhd->khd", d_scores, query_blk, preferred_element_type=jnp.float32)
            * score_scale
        )
        d_value = d_value + jnp.einsum(
            "hqk,qhd->khd", prob_bf16, d_out, preferred_element_type=jnp.float32
        )
        return ((d_key, d_value), d_query)

    zero_keys = jnp.zeros((group_rows, local_heads, head_dim), jnp.float32)
    (d_key, d_value), d_query = lax.scan(
        backward_block,
        (zero_keys, zero_keys),
        (query_blocks, seg_blocks, pos_blocks, log_total, d_blocks),
    )
    owned_grads = lax.psum_scatter(
        jnp.stack([d_key, d_value], axis=1), "blk", scatter_dimension=0, tiled=True
    )
    grads_heads = jnp.concatenate(
        [d_query.reshape(shard_rows, 1, local_heads, head_dim), owned_grads], axis=1
    ).astype(jnp.bfloat16)
    cot_sums = jnp.sum(cotangent, axis=0, dtype=jnp.float32)
    d_linear = rotary_back(grads_heads.astype(jnp.float32))[0].reshape(shard_rows, 3 * col_width)
    d_linear_bf16 = d_linear.astype(jnp.bfloat16)
    d_one_terms = lax.dot_general(
        d_linear_bf16, qkv_cols, contract_last, preferred_element_type=jnp.float32
    )
    d_norm_one, d_norm_two = (
        lax.psum_scatter(d_one_terms, "head", scatter_dimension=0, tiled=True),
        lax.psum_scatter(d_two_terms, "head", scatter_dimension=0, tiled=True),
    )
    group_block = model_width // weight_owners
    block_sum = lax.psum_scatter(
        jnp.concatenate(
            [
                lax.dot_general(
                    attn_rows, d_linear_bf16, contract_rows, preferred_element_type=jnp.float32
                ),
                lax.dot_general(
                    attn_full, cot_cols, contract_rows, preferred_element_type=jnp.float32
                ),
                lax.dot_general(
                    mlp_rows, d_up_bf16, contract_rows, preferred_element_type=jnp.float32
                ),
                lax.dot_general(
                    cot_rows, act_bf16, contract_rows, preferred_element_type=jnp.float32
                ),
            ],
            axis=1,
        ),
        ("dp", "blk"),
        scatter_dimension=0,
        tiled=True,
    )
    part_qkv = block_sum[:, : 3 * col_width].reshape(group_block, 3, 1, col_width)
    part_out = block_sum[:, 3 * col_width : 4 * col_width].reshape(group_block, 1, 1, col_width)
    part_up = block_sum[:, 4 * col_width : 4 * col_width + ff_cols].reshape(
        group_block, 1, 1, ff_cols
    )
    part_down = block_sum[:, 4 * col_width + ff_cols :].reshape(group_block, 1, 1, ff_cols)
    owned_qkv, owned_out, owned_up, owned_down = (
        lax.all_to_all(part_qkv, "head", split_axis=0, concat_axis=2, tiled=True),
        lax.all_to_all(part_out, "head", split_axis=0, concat_axis=2, tiled=True),
        lax.all_to_all(part_up, "head", split_axis=0, concat_axis=2, tiled=True),
        lax.all_to_all(part_down, "head", split_axis=0, concat_axis=2, tiled=True),
    )
    grad_w_qkv = owned_qkv.reshape(owner_rows, 3 * model_width)
    grad_w_out = owned_out.reshape(owner_rows, model_width)
    grad_w_up = owned_up.reshape(owner_rows, hidden_units)
    grad_w_down = owned_down.reshape(owner_rows, hidden_units)
    selector = (jnp.arange(head_count, dtype=jnp.int32) == head_index).astype(jnp.float32)
    linear_sums = jnp.sum(d_linear_bf16, axis=0, dtype=jnp.float32).reshape(3, col_width)
    qkv_sums = (linear_sums[:, None, :] * selector[None, :, None]).reshape(3 * model_width)
    up_local = jnp.sum(d_up_bf16, axis=0, dtype=jnp.float32)
    up_sums = (up_local[None, :] * selector[:, None]).reshape(hidden_units)
    d_from_one, gain_one, shift_one = norm_back_one(d_norm_one)
    d_from_two, gain_two, shift_two = norm_back_two(d_norm_two)
    d_tokens = cot_f32 + d_from_one + d_from_two
    small_sums = lax.psum(
        (gain_one, shift_one, gain_two, shift_two, qkv_sums, cot_sums, up_sums),
        ("dp", "blk", "head"),
    )
    return (
        block_output,
        d_tokens,
        small_sums[0],
        small_sums[1],
        small_sums[2],
        small_sums[3],
        grad_w_qkv,
        small_sums[4],
        grad_w_out,
        small_sums[5],
        grad_w_up,
        small_sums[6],
        grad_w_down,
        small_sums[5],
    )


RUN = 256
TILE = 512
PLANE = ("blk", "head")
ALL = ("dp", "blk", "head")
NT = (((1,), (1,)), ((), ()))
TN = (((0,), (0,)), ((), ()))


def turn(part, cosine, sine):
    lane = lax.broadcasted_iota(jnp.int32, part.shape, 1)
    half = ROT // 2
    other = jnp.where(lane < half, pltpu.roll(part, 128 - half, 1), pltpu.roll(part, half, 1))
    return part * cosine + other * sine


def fold_rows(value):
    return value.reshape(value.shape[0] // 8, 8, value.shape[1])


def attention_kernel(
    order_ref,
    lin_a,
    lin_b,
    cot_a,
    cot_b,
    cos_ref,
    sin_ref,
    out_ref,
    dlin_ref,
    sums_ref,
    q_c,
    k_c,
    v_c,
    d_c,
    kt_c,
    vt_c,
    dk_c,
    dv_c,
    s_c,
    p_c,
    ot_c,
):
    step = pl.program_id(0)
    prompt_tiles = (RUN * 8) // TILE
    f32 = jnp.float32
    bf16 = jnp.bfloat16

    @pl.when(step == 0)
    def _():
        sums_ref[...] = jnp.zeros_like(sums_ref)

    for side, (lin, cot) in enumerate(((lin_a, cot_a), (lin_b, cot_b))):
        run = step * 2 + side
        rows = pl.ds(pl.multiple_of(run * RUN, RUN), RUN)
        table = jnp.minimum(run, 8)
        cosine = cos_ref[table]
        sine = sin_ref[table]
        for part, target in ((0, q_c), (1, k_c)):
            base = part * HD
            turned = turn(lin[:, base : base + 128], cosine, sine)
            whole = jnp.concatenate([turned, lin[:, base + 128 : base + HD]], axis=1).astype(bf16)
            if part == 0:
                target[rows, :] = whole * jnp.asarray(HD**-0.5, bf16)
            else:
                target[rows, :] = whole
                kt_c[:, rows] = whole.T
        value = lin[:, 2 * HD :].astype(bf16)
        v_c[rows, :] = value
        vt_c[:, rows] = value.T
        d_c[rows, :] = cot[...]

    def rows_of(tile):
        return pl.ds(pl.multiple_of(tile * TILE, TILE), TILE)

    own = rows_of(step)
    query = q_c[own, :]
    d_out = d_c[own, :]
    before = jnp.minimum(step, prompt_tiles)

    def scores_of(tile):
        return lax.dot_general(k_c[rows_of(tile), :], query, NT, preferred_element_type=f32)

    def first(tile, top):
        scores = scores_of(tile)
        s_c[tile] = scores
        return jnp.maximum(top, jnp.max(fold_rows(scores), axis=0))

    key_row = lax.broadcasted_iota(jnp.int32, (TILE, TILE), 0)
    query_col = lax.broadcasted_iota(jnp.int32, (TILE, TILE), 1)
    same_run = (key_row // RUN) == (query_col // RUN)
    seen = (key_row <= query_col) & (same_run | (step < prompt_tiles))
    masked = jnp.where(seen, scores_of(step), -1e30)
    s_c[prompt_tiles] = masked
    top = lax.fori_loop(0, before, first, jnp.max(fold_rows(masked), axis=0))
    top = jnp.max(top, axis=0, keepdims=True)

    def second(slot, tile, carry):
        total, inner = carry
        grown = jnp.exp(s_c[slot] - top)
        s_c[slot] = grown
        d_prob = lax.dot_general(v_c[rows_of(tile), :], d_out, NT, preferred_element_type=f32)
        p_c[slot] = d_prob
        add = jnp.dot(vt_c[:, rows_of(tile)], grown.astype(bf16), preferred_element_type=f32)
        return (
            total + jnp.sum(fold_rows(grown), axis=0),
            inner + jnp.sum(fold_rows(grown * d_prob), axis=0),
            add,
        )

    zero = jnp.zeros((8, TILE), f32)
    total, inner, add = second(prompt_tiles, step, (zero, zero))
    ot_c[...] = add

    def second_loop(tile, carry):
        total, inner, add = second(tile, tile, carry)
        ot_c[...] += add
        return (total, inner)

    total, inner = lax.fori_loop(0, before, second_loop, (total, inner))
    scale = 1.0 / jnp.sum(total, axis=0, keepdims=True)
    inner = jnp.sum(inner, axis=0, keepdims=True) * scale
    attended = (ot_c[...] * scale).astype(bf16).T

    def third(slot, tile):
        prob = s_c[slot] * scale
        d_value = jnp.dot(prob.astype(bf16), d_out, preferred_element_type=f32)
        d_score = (prob * (p_c[slot] - inner)).astype(bf16)
        d_key = jnp.dot(d_score, query, preferred_element_type=f32)
        d_query = jnp.dot(kt_c[:, rows_of(tile)], d_score, preferred_element_type=f32)
        return d_value, d_key, d_query

    d_value, d_key, d_query = third(prompt_tiles, step)
    dv_c[own, :] = d_value
    dk_c[own, :] = d_key
    ot_c[...] = d_query

    def third_loop(tile, carry):
        d_value, d_key, d_query = third(tile, tile)
        dv_c[rows_of(tile), :] += d_value
        dk_c[rows_of(tile), :] += d_key
        ot_c[...] += d_query
        return carry

    lax.fori_loop(0, before, third_loop, 0)
    d_query = (ot_c[...] * HD**-0.5).T

    def put(run, part, grad):
        table = jnp.minimum(run, 8)
        turned = turn(grad[:, :128], cos_ref[table], -sin_ref[table])
        whole = jnp.concatenate([turned, grad[:, 128:]], axis=1) if part < 2 else grad
        whole = whole.astype(bf16)
        columns = slice(part * HD, part * HD + HD)
        dlin_ref[pl.ds(pl.multiple_of(order_ref[run] * RUN, RUN), RUN), columns] = whole
        sums_ref[:, columns] += jnp.sum(fold_rows(whole.astype(f32)), axis=0)

    for side in range(2):
        run = step * 2 + side
        piece = slice(side * RUN, side * RUN + RUN)
        put(run, 0, d_query[piece])
        out_ref[pl.ds(pl.multiple_of(order_ref[run] * RUN, RUN), RUN), :] = attended[piece]

    @pl.when(step == pl.num_programs(0) - 1)
    def _():
        def finish(run, carry):
            rows = pl.ds(pl.multiple_of(run * RUN, RUN), RUN)
            put(run, 1, dk_c[rows, :])
            put(run, 2, dv_c[rows, :])
            return carry

        lax.fori_loop(0, 2 * pl.num_programs(0), finish, 0)


def attention(order, linear, d_attn, cosine, sine):
    rows = linear.shape[0]
    bf16, f32 = jnp.bfloat16, jnp.float32
    whole = lambda shape: pl.BlockSpec(
        shape, lambda i, o: (0,) * len(shape), pipeline_mode=pl.Buffered(1)
    )
    run_of = lambda side, width: pl.BlockSpec((RUN, width), lambda i, o: (o[2 * i + side], 0))
    slots = (RUN * 8) // TILE + 1
    return pl.pallas_call(
        attention_kernel,
        out_shape=(
            jax.ShapeDtypeStruct((rows, HD), bf16),
            jax.ShapeDtypeStruct((rows, 3 * HD), bf16),
            jax.ShapeDtypeStruct((8, 3 * HD), f32),
        ),
        grid_spec=pltpu.PrefetchScalarGridSpec(
            num_scalar_prefetch=1,
            grid=(rows // TILE,),
            in_specs=[
                run_of(0, 3 * HD),
                run_of(1, 3 * HD),
                run_of(0, HD),
                run_of(1, HD),
                whole(cosine.shape),
                whole(sine.shape),
            ],
            out_specs=[whole((rows, HD)), whole((rows, 3 * HD)), whole((8, 3 * HD))],
            scratch_shapes=[pltpu.VMEM((rows, HD), bf16)] * 4
            + [pltpu.VMEM((HD, rows), bf16)] * 2
            + [pltpu.VMEM((rows, HD), f32)] * 2
            + [pltpu.VMEM((slots, TILE, TILE), f32)] * 2
            + [pltpu.VMEM((HD, TILE), f32)],
        ),
        compiler_params=pltpu.CompilerParams(
            dimension_semantics=("arbitrary",), vmem_limit_bytes=60 << 20
        ),
        cost_estimate=pl.CostEstimate(
            flops=24_000_000_000, transcendentals=8_000_000, bytes_accessed=24_000_000
        ),
    )(order, linear, linear, d_attn, d_attn, cosine, sine)


def swap(value, bits):
    plane = lax.axis_size(PLANE)
    return lax.ppermute(value, PLANE, [(p, p ^ bits) for p in range(plane)])


def norm_kernel(x_ref, scale_ref, *refs):
    attn_ref, mlp_ref = refs[-2:]
    value = x_ref[...].astype(jnp.float32)
    centered = value - jnp.mean(value, axis=-1, keepdims=True)
    variance = jnp.mean(centered * centered, axis=-1, keepdims=True)
    normed = centered * lax.rsqrt(variance + 1e-05)
    attn_ref[...] = (normed * scale_ref[0:1, :] + scale_ref[1:2, :]).astype(jnp.bfloat16)
    mlp_ref[...] = (normed * scale_ref[2:3, :] + scale_ref[3:4, :]).astype(jnp.bfloat16)


def norm_into(block, scales, filled, first, total):
    count, width = block.shape
    step = 256
    spec = pl.BlockSpec((step, width), lambda i: (first // step + i, 0))
    shape = jax.ShapeDtypeStruct((total, width), jnp.bfloat16)
    kept = pl.BlockSpec(memory_space=pl.ANY)
    return pl.pallas_call(
        norm_kernel,
        out_shape=(shape, shape),
        grid=(count // step,),
        in_specs=[
            pl.BlockSpec((step, width), lambda i: (i, 0)),
            pl.BlockSpec(scales.shape, lambda i: (0, 0)),
        ]
        + [kept] * len(filled),
        out_specs=(spec, spec),
        input_output_aliases={2: 0, 3: 1} if filled else {},
        cost_estimate=pl.CostEstimate(
            flops=12 * count * width, transcendentals=count, bytes_accessed=6 * count * width
        ),
    )(block, scales, *filled)


def after(value, *others):
    return lax.optimization_barrier((value, *others))[0]


def total_of(value, axis_bits, axes):
    for bits in axis_bits:
        count = lax.axis_size(axes)
        value = value + lax.ppermute(value, axes, [(p, p ^ bits) for p in range(count)])
    return value


def shards_by_heads(
    tokens,
    cotangent,
    segment,
    position,
    ln1_gain,
    ln1_bias,
    ln2_gain,
    ln2_bias,
    w_qkv,
    b_qkv,
    w_out,
    b_out,
    w_up,
    b_up,
    w_down,
    b_down,
):
    bf16, f32 = jnp.bfloat16, jnp.float32
    rows, width = tokens.shape
    hidden = w_up.shape[1]
    planes = lax.axis_size("dp")
    plane = lax.axis_size(PLANE)
    z_at = lax.axis_index("dp")
    p_at = lax.axis_index(PLANE)
    owned = w_qkv.shape[0]
    slice_ff = hidden // plane
    first = (z_at * plane + p_at) * owned

    marks = jnp.stack([segment[::RUN], position[::RUN]], axis=1)
    marks = jnp.pad(marks, ((0, 8 - marks.shape[0]), (0, 126)))

    def to_columns(weight):
        sent = lax.all_to_all(weight.transpose(1, 0, 2), PLANE, split_axis=0, concat_axis=0, tiled=True)
        return sent.reshape(plane * owned, weight.shape[2])

    half = rows // 2
    total = plane * rows
    scales = jnp.pad(jnp.stack([ln1_gain, ln1_bias, ln2_gain, ln2_bias]), ((0, 4), (0, 0)))
    tok_x, tok_y = swap(tokens, 4), swap(tokens, 1)
    up_cols = to_columns(w_up.reshape(owned, plane, slice_ff))
    qkv_own = w_qkv.reshape(owned, 3, plane, HD).transpose(0, 2, 1, 3).reshape(owned, plane, 3 * HD)
    qkv_cols = to_columns(after(qkv_own, tok_x, tok_y, up_cols))
    tok_far, tok_far_too = swap(tok_y[:half], 4), swap(tok_x[half:], 1)
    near = [tokens, tok_x, tok_y, tok_far, tok_far_too]
    inputs = ()
    for piece, place in zip(near, (0, rows, 2 * rows, 3 * rows, 3 * rows + half)):
        inputs = norm_into(piece, scales, inputs, place, total)
        inputs = norm_into(swap(piece, 2), scales, inputs, place + 4 * rows, total)
    a_all, m_all = inputs
    cot_sent = after(cotangent, qkv_cols, tok_far, tok_far_too)
    cot_x, cot_y = swap(cot_sent, 4), swap(cot_sent, 1)
    cot_sums = jnp.sum(cot_sent, axis=0, dtype=f32)

    w_ff = lax.all_gather(up_cols, "dp", axis=0, tiled=True)
    head_out = jnp.concatenate([qkv_cols, w_out.reshape(plane * owned, width // plane)], axis=1)
    head_out = lax.all_gather(head_out, "dp", axis=0, tiled=True)
    w_head = head_out[:, : 3 * HD]
    out_rows = head_out[:, 3 * HD :].reshape(planes, owned, width)

    parts = HD // owned
    per_plane = HEADS // planes

    def to_head(turn_at):
        return [(p, per_plane * ((p % parts - turn_at) % parts) + p // parts) for p in range(plane)]

    w_o = jnp.zeros((parts, owned, width), bf16)
    for turn_at in range(parts):
        piece = lax.dynamic_index_in_dim(out_rows, (p_at % parts - turn_at) % parts, 0, keepdims=False)
        got = lax.ppermute(piece, PLANE, to_head(turn_at))
        w_o = lax.dynamic_update_index_in_dim(w_o, got, (turn_at + p_at // per_plane) % parts, 0)
    w_o = w_o.reshape(HD, width)
    lane = lax.broadcasted_iota(jnp.int32, (9 * RUN, 128), 1)
    place = lax.broadcasted_iota(jnp.int32, (9 * RUN, 128), 0).astype(f32)
    pairs = ROT // 2
    frequency = jnp.exp((lane % pairs).astype(f32) * (-2.0 * math.log(10000.0) / ROT))
    angle = place * frequency
    cosine = jnp.where(lane < ROT, jnp.cos(angle), 1.0).reshape(9, RUN, 128)
    sine = jnp.where(lane < pairs, -jnp.sin(angle), jnp.sin(angle))
    sine = jnp.where(lane < ROT, sine, 0.0).reshape(9, RUN, 128)

    w_ff = after(w_ff, cosine, sine)
    b_ff = lax.dynamic_slice_in_dim(b_up, p_at * slice_ff, slice_ff)
    up_linear = jnp.dot(m_all, w_ff, preferred_element_type=f32) + b_ff
    below = 0.5 + 0.5 * lax.erf(up_linear * (0.5**0.5))
    act = (up_linear * below).astype(bf16)
    slope = below + up_linear * jnp.exp(-0.5 * up_linear * up_linear) * ((2.0 * math.pi) ** -0.5)
    act, slope = lax.optimization_barrier((act, slope.astype(bf16)))

    cot_own, cot_x, cot_y = lax.optimization_barrier((cot_sent, cot_x, cot_y, act))[:3]
    cot_far, cot_far_too = swap(cot_y[:half], 4), swap(cot_x[half:], 1)
    near = [cot_own, cot_x, cot_y, cot_far, cot_far_too]
    cot_all = jnp.concatenate(near + [swap(piece, 2) for piece in near], axis=0)
    marks = swap_marks(after(marks, cot_far, cot_far_too))
    seg_run, pos_run = marks[:, 0], marks[:, 1]
    rank = jnp.where(seg_run == 0, pos_run // RUN, seg_run + 7)
    order = jnp.argsort(rank).astype(jnp.int32)
    down_cols = to_columns(after(w_down.reshape(owned, plane, slice_ff), cot_far, cot_far_too))
    w_dn = lax.all_gather(down_cols, "dp", axis=0, tiled=True)

    def summed(grad):
        return lax.psum_scatter(grad, "dp", scatter_dimension=0, tiled=True)

    def owner_rows(grad):
        back = lax.all_to_all(grad.reshape(plane, owned, -1), PLANE, split_axis=0, concat_axis=0, tiled=True)
        return back.astype(f32)

    def grad_of(left, right):
        return lax.dot_general(left, right, TN, preferred_element_type=f32)

    def plane_sum(terms):
        def plus(value, *added):
            for more in added:
                value = value + more.astype(f32)
            return value.astype(bf16)

        def start(*late):
            return plus(terms(late, 4 * rows, 8 * rows))

        def far(other, *late):
            mine = plus(terms(late, 3 * rows, 4 * rows), other[3 * rows :])
            return mine, swap(mine[:half], 4), swap(mine[half:], 1)

        def sides(other, far_y, far_x, *late):
            far_x = jnp.pad(far_x, ((half, 0), (0, 0)))
            far_y = jnp.pad(far_y, ((0, half), (0, 0)))
            to_x = plus(terms(late, rows, 2 * rows), other[rows : 2 * rows], far_x)
            to_y = plus(terms(late, 2 * rows, 3 * rows), other[2 * rows : 3 * rows], far_y)
            return to_x, to_y, swap(to_x, 4), swap(to_y, 1)

        def finish(other, got_x, got_y, *late):
            value = terms(late, 0, rows) + other[:rows].astype(f32)
            return value + got_x.astype(f32) + got_y.astype(f32)

        return start, far, sides, finish

    b_head = lax.dynamic_index_in_dim(b_qkv.reshape(3, plane, HD), p_at, 1, keepdims=False)
    g_down = grad_of(cot_all, act).astype(bf16)
    linear = jnp.dot(a_all, after(w_head, g_down), preferred_element_type=f32) + b_head.reshape(3 * HD)
    d_attn = lax.dot_general(cot_all, w_o, NT, preferred_element_type=f32).astype(bf16)
    attn, d_linear, head_sums = attention(order, linear, d_attn, cosine, sine)
    g_down = summed(g_down)

    z_head = grad_of(a_all, d_linear)
    z_low = z_head.astype(bf16)
    g_out = grad_of(after(attn, z_low), cot_all).astype(bf16).reshape(parts, owned, width)
    out_parts = jnp.zeros((parts, owned, width), bf16)
    for turn_at in range(parts):
        piece = lax.dynamic_index_in_dim(g_out, (turn_at + p_at // per_plane) % parts, 0, keepdims=False)
        got = lax.ppermute(piece, PLANE, [(b, a) for a, b in to_head(turn_at)])
        out_parts = lax.dynamic_update_index_in_dim(out_parts, got, (p_at % parts - turn_at) % parts, 0)
    head_sum = jnp.concatenate([z_low, out_parts.reshape(width, HD)], axis=1)
    head_sum = summed(head_sum)

    branch_in = jnp.concatenate([attn, act], axis=1)
    branch_w = jnp.concatenate([w_o, w_dn.T], axis=0)
    b_start, b_far, b_sides, b_finish = plane_sum(
        lambda late, i, j: jnp.dot(after(branch_in, *late)[i:j], branch_w, preferred_element_type=f32)
    )
    b_terms = b_start(g_out)
    b_other = swap(b_terms, 2)

    d_act = jnp.dot(cot_all, after(w_dn, b_terms, out_parts), preferred_element_type=f32)
    d_up = (d_act * slope.astype(f32)).astype(bf16)
    far_terms, far_y, far_x = b_far(b_other, d_up)

    d_in = jnp.concatenate([d_linear, d_up], axis=1)
    d_w = jnp.concatenate(
        [
            (w_head.astype(f32) * ln1_gain[:, None]).astype(bf16),
            (w_ff.astype(f32) * ln2_gain[:, None]).astype(bf16),
        ],
        axis=1,
    )
    p_start, p_far, p_sides, p_finish = plane_sum(
        lambda late, i, j: lax.dot_general(
            after(d_in, *late)[i:j], d_w, NT, preferred_element_type=f32
        )
    )
    p_terms = p_start(far_terms)
    p_other = swap(p_terms, 2)
    to_x, to_y, b_x, b_y = b_sides(b_other, far_y, far_x, p_terms)
    far_terms, far_y, far_x = p_far(p_other, to_x, to_y)
    z_ff = grad_of(m_all, after(d_up, far_terms))
    z_up = z_ff.astype(bf16)
    z_up_sum = summed(z_up)
    branch = b_finish(b_other, b_x, b_y, z_up)
    block_output = (tokens.astype(f32) + branch + (b_out + b_down)).astype(bf16)
    to_x, to_y, p_x, p_y = p_sides(p_other, far_y, far_x, block_output)
    pulled = p_finish(p_other, p_x, p_y, to_x, to_y)
    tokens_f32 = tokens.astype(f32)
    centered = tokens_f32 - jnp.mean(tokens_f32, axis=-1, keepdims=True)
    spread = lax.rsqrt(jnp.mean(centered * centered, axis=-1, keepdims=True) + 1e-05)
    normed = centered * spread
    d_tokens = cotangent.astype(f32) + spread * (
        pulled
        - jnp.mean(pulled, axis=-1, keepdims=True)
        - normed * jnp.mean(pulled * normed, axis=-1, keepdims=True)
    )

    head_sums = jnp.sum(head_sums, axis=0)
    ff_sums = jnp.sum(d_up, axis=0, dtype=f32)
    shift_head = jnp.sum(w_head.astype(f32) * head_sums, axis=1)
    shift_ff = jnp.sum(w_ff.astype(f32) * ff_sums, axis=1)
    gain_head = (jnp.sum(z_head * w_head.astype(f32), axis=1) - ln1_bias * shift_head) / ln1_gain
    gain_ff = (jnp.sum(z_ff * w_ff.astype(f32), axis=1) - ln2_bias * shift_ff) / ln2_gain
    gain_head = after(gain_head, to_x, to_y)
    small = jnp.concatenate([gain_head, shift_head, gain_ff, shift_ff, cot_sums]).reshape(-1, 128)
    sums = jnp.concatenate([head_sums, ff_sums]).reshape(-1, 128)
    count = sums.shape[0]
    both = total_of(jnp.concatenate([sums, small], axis=0), (1, 2), "dp")
    sums, small = both[:count], both[count:]
    sums = lax.dynamic_update_slice_in_dim(jnp.zeros((plane * count, 128), f32), sums, p_at * count, 0)
    both = total_of(jnp.concatenate([sums, small], axis=0), (1, 4, 2), PLANE)
    sums, small = both[: plane * count].reshape(plane, count * 128), both[plane * count :].reshape(5, width)
    grad_b_qkv = sums[:, : 3 * HD].reshape(plane, 3, HD).transpose(1, 0, 2).reshape(3 * width)
    grad_b_up = sums[:, 3 * HD :].reshape(hidden)

    z_qkv = owner_rows(head_sum[:, : 3 * HD]).reshape(plane, owned, 3, HD).transpose(1, 2, 0, 3)
    grad_w_qkv = z_qkv.reshape(owned, 3 * width)
    grad_w_up = owner_rows(z_up_sum).transpose(1, 0, 2).reshape(owned, hidden)
    grad_w_down = owner_rows(g_down).transpose(1, 0, 2).reshape(owned, hidden)
    grad_w_out = head_sum[:, 3 * HD :].reshape(owned, width).astype(f32)
    return (
        block_output,
        d_tokens,
        small[0],
        small[1],
        small[2],
        small[3],
        grad_w_qkv,
        grad_b_qkv,
        grad_w_out,
        small[4],
        grad_w_up,
        grad_b_up,
        grad_w_down,
        small[4],
    )


def swap_marks(marks):
    mine = marks[:2]
    got = swap(marks, 4)[:2]
    pair = jnp.concatenate([mine, got], axis=0)
    pair = jnp.pad(pair, ((0, 4), (0, 0)))
    four = jnp.concatenate([pair[:4], swap(pair, 1)[:4]], axis=0)
    return jnp.concatenate([four, swap(four, 2)], axis=0)


def solution(mesh):
    plane = mesh.shape["blk"] * mesh.shape["head"]
    body = shards_by_heads if plane == HEADS else shards_by_blocks
    placed = (
        P(("dp", "blk", "head"), None),
        P(("dp", "blk", "head"), None),
        P(("dp", "blk", "head")),
        P(("dp", "blk", "head")),
        P(),
        P(),
        P(),
        P(),
        P(("dp", "blk", "head"), None),
        P(),
        P(("dp", "blk", "head"), None),
        P(),
        P(("dp", "blk", "head"), None),
        P(),
        P(("dp", "blk", "head"), None),
        P(),
    )
    return jax.shard_map(
        body,
        mesh=mesh,
        in_specs=placed,
        out_specs=(
            P(("dp", "blk", "head"), None),
            P(("dp", "blk", "head"), None),
            P(),
            P(),
            P(),
            P(),
            P(("dp", "blk", "head"), None),
            P(),
            P(("dp", "blk", "head"), None),
            P(),
            P(("dp", "blk", "head"), None),
            P(),
            P(("dp", "blk", "head"), None),
            P(),
        ),
        check_vma=False,
    )
```

```python
from functools import partial
import math

import jax
import jax.numpy as jnp
from jax import lax
from jax.experimental import pallas as pl
from jax.experimental.pallas import tpu as pltpu
from jax.sharding import PartitionSpec as P


HEADS = 8
HD = 256
ROT = 64


def layer_norm(values, norm_gain, norm_bias):
    average = jnp.mean(values, axis=-1, keepdims=True)
    centered = values - average
    variance = jnp.mean(centered * centered, axis=-1, keepdims=True)
    return centered * lax.rsqrt(variance + 1e-05) * norm_gain + norm_bias


def rotate(tensor, positions):
    half_dims = ROT // 2
    frequency = jnp.exp(jnp.arange(half_dims, dtype=jnp.float32) * (-2.0 * math.log(10000.0) / ROT))
    angles = positions.astype(jnp.float32)[:, None] * frequency[None, :]
    cosine = jnp.cos(angles)[:, None, :]
    sine_val = jnp.sin(angles)[:, None, :]
    first_half = tensor[..., :half_dims]
    second_half = tensor[..., half_dims:ROT]
    untouched = tensor[..., ROT:]
    return jnp.concatenate(
        [
            first_half * cosine - second_half * sine_val,
            second_half * cosine + first_half * sine_val,
            untouched,
        ],
        axis=-1,
    )


def rotate_parts(linear, positions):
    return jnp.stack(
        [rotate(linear[:, 0], positions), rotate(linear[:, 1], positions), linear[:, 2]], axis=1
    )


def visible(seg_q, pos_q, seg_k, pos_k):
    same_seg = seg_q[:, None] == seg_k[None, :]
    causal = pos_k[None, :] <= pos_q[:, None]
    prompt_key = (seg_k[None, :] == 0) & (seg_q[:, None] != 0)
    return same_seg & causal | prompt_key


def shards_by_blocks(
    tokens,
    cotangent,
    segment,
    position,
    ln1_gain,
    ln1_bias,
    ln2_gain,
    ln2_bias,
    w_qkv,
    b_qkv,
    w_out,
    b_out,
    w_up,
    b_up,
    w_down,
    b_down,
):
    tok_rows = tokens.shape[0]
    model_width = tokens.shape[1]
    hidden_units = w_up.shape[1]
    head_dim = HD
    head_count = lax.axis_size("head")
    local_heads = HEADS // head_count
    col_width = model_width // head_count
    ff_cols = hidden_units // head_count
    head_index = lax.axis_index("head")
    weight_owners = lax.axis_size("dp") * lax.axis_size("blk")
    owner_rows = w_qkv.shape[0]
    contract_last = (((1,), (1,)), ((), ()))
    contract_rows = (((0,), (0,)), ((), ()))
    row_seg, row_pos = (
        lax.all_gather(segment, ("blk", "head"), axis=0, tiled=True),
        lax.all_gather(position, ("blk", "head"), axis=0, tiled=True),
    )
    shard_rows = tok_rows * head_count
    first_row = lax.axis_index("blk") * shard_rows
    seg_local = lax.dynamic_slice_in_dim(row_seg, first_row, shard_rows)
    pos_local = lax.dynamic_slice_in_dim(row_pos, first_row, shard_rows)
    tokens_f32 = tokens.astype(jnp.float32)
    cot_f32 = cotangent.astype(jnp.float32)
    normed_one, norm_back_one = jax.vjp(layer_norm, tokens_f32, ln1_gain, ln1_bias)
    attn_input = normed_one.astype(jnp.bfloat16)
    normed_two, norm_back_two = jax.vjp(layer_norm, tokens_f32, ln2_gain, ln2_bias)
    mlp_input = normed_two.astype(jnp.bfloat16)
    qkv_parts = w_qkv.reshape(owner_rows, 3, head_count, col_width)
    out_parts = w_out.reshape(owner_rows, 1, head_count, col_width)
    up_parts = w_up.reshape(owner_rows, 1, head_count, ff_cols)
    down_parts = w_down.reshape(owner_rows, 1, head_count, ff_cols)
    slice_qkv, slice_out, slice_up, slice_down = (
        lax.all_to_all(qkv_parts, "head", split_axis=2, concat_axis=0, tiled=True),
        lax.all_to_all(out_parts, "head", split_axis=2, concat_axis=0, tiled=True),
        lax.all_to_all(up_parts, "head", split_axis=2, concat_axis=0, tiled=True),
        lax.all_to_all(down_parts, "head", split_axis=2, concat_axis=0, tiled=True),
    )
    whole_qkv, whole_out, whole_up, whole_down = (
        lax.all_gather(slice_qkv, ("dp", "blk"), axis=0, tiled=True),
        lax.all_gather(slice_out, ("dp", "blk"), axis=0, tiled=True),
        lax.all_gather(slice_up, ("dp", "blk"), axis=0, tiled=True),
        lax.all_gather(slice_down, ("dp", "blk"), axis=0, tiled=True),
    )
    qkv_cols = whole_qkv.reshape(model_width, 3 * col_width)
    out_cols = whole_out.reshape(model_width, col_width)
    up_cols = whole_up.reshape(model_width, ff_cols)
    down_cols = whole_down.reshape(model_width, ff_cols)
    attn_rows, mlp_rows, cot_rows = (
        lax.all_gather(attn_input, "head", axis=0, tiled=True),
        lax.all_gather(mlp_input, "head", axis=0, tiled=True),
        lax.all_gather(cotangent, "head", axis=0, tiled=True),
    )
    bias_local = lax.dynamic_index_in_dim(
        b_qkv.reshape(3, head_count, col_width), head_index, 1, keepdims=False
    ).reshape(3 * col_width)
    qkv_linear = jnp.dot(attn_rows, qkv_cols, preferred_element_type=jnp.float32) + bias_local
    qkv_split = qkv_linear.reshape(shard_rows, 3, local_heads, head_dim)
    rotated, rotary_back = jax.vjp(lambda linear: rotate_parts(linear, pos_local), qkv_split)
    by_head = rotated.astype(jnp.bfloat16)
    queries = by_head[:, 0]
    keys_vals = lax.all_gather(by_head[:, 1:], "blk", axis=0, tiled=True)
    keys_all = keys_vals[:, 0]
    values_all = keys_vals[:, 1]
    group_rows = keys_all.shape[0]
    score_rows = math.gcd(shard_rows, 512)
    block_count = shard_rows // score_rows
    score_scale = head_dim ** (-0.5)
    query_blocks = queries.reshape(block_count, score_rows, local_heads, head_dim)
    seg_blocks = seg_local.reshape(block_count, score_rows)
    pos_blocks = pos_local.reshape(block_count, score_rows)

    def scores_of(query_blk, seg_blk, pos_blk):
        raw_scores = (
            jnp.einsum("qhd,khd->hqk", query_blk, keys_all, preferred_element_type=jnp.float32)
            * score_scale
        )
        visible_mask = visible(seg_blk, pos_blk, row_seg, row_pos)[None]
        return jnp.where(visible_mask, raw_scores, -1e30)

    def forward_block(inputs):
        query_blk, seg_blk, pos_blk = inputs
        scores = scores_of(query_blk, seg_blk, pos_blk)
        row_max = jnp.max(scores, axis=-1, keepdims=True)
        unnormed = jnp.exp(scores - row_max)
        row_sum = jnp.sum(unnormed, axis=-1, keepdims=True)
        prob_bf16 = (unnormed / row_sum).astype(jnp.bfloat16)
        attended = jnp.einsum(
            "hqk,khd->qhd", prob_bf16, values_all, preferred_element_type=jnp.float32
        )
        return (attended, (row_max + jnp.log(row_sum))[..., 0])

    attended_all, log_total = lax.map(forward_block, (query_blocks, seg_blocks, pos_blocks))
    attn_heads = attended_all.reshape(shard_rows, local_heads, head_dim).astype(jnp.bfloat16)
    attn_full = lax.all_gather(
        attn_heads.reshape(shard_rows, col_width), "head", axis=1, tiled=True
    )
    out_bias = lax.dynamic_slice_in_dim(b_out, head_index * col_width, col_width)
    branch_cols = jnp.dot(attn_full, out_cols, preferred_element_type=jnp.float32) + out_bias
    attn_branch = lax.all_to_all(branch_cols, "head", split_axis=0, concat_axis=1, tiled=True)
    up_bias = lax.dynamic_slice_in_dim(b_up, head_index * ff_cols, ff_cols)
    up_linear = jnp.dot(mlp_rows, up_cols, preferred_element_type=jnp.float32) + up_bias
    activation, gelu_back = jax.vjp(partial(jax.nn.gelu, approximate=False), up_linear)
    act_bf16 = activation.astype(jnp.bfloat16)
    mlp_terms = lax.dot_general(
        act_bf16, down_cols, contract_last, preferred_element_type=jnp.float32
    )
    mlp_branch = lax.psum_scatter(
        mlp_terms.astype(jnp.bfloat16), "head", scatter_dimension=0, tiled=True
    ).astype(jnp.float32)
    block_output = (tokens_f32 + attn_branch + mlp_branch + b_down).astype(jnp.bfloat16)
    d_act = jnp.dot(cot_rows, down_cols, preferred_element_type=jnp.float32)
    d_up_bf16 = gelu_back(d_act)[0].astype(jnp.bfloat16)
    d_two_terms = lax.dot_general(
        d_up_bf16, up_cols, contract_last, preferred_element_type=jnp.float32
    )
    cot_cols = lax.dynamic_slice_in_dim(cot_rows, head_index * col_width, col_width, 1)
    d_attn_terms = lax.dot_general(
        cot_cols, out_cols, contract_last, preferred_element_type=jnp.float32
    )
    d_attn_sum = lax.psum_scatter(d_attn_terms, "head", scatter_dimension=1, tiled=True)
    d_heads = d_attn_sum.astype(jnp.bfloat16).reshape(shard_rows, local_heads, head_dim)
    d_blocks = d_heads.reshape(block_count, score_rows, local_heads, head_dim)

    def backward_block(carried, inputs):
        d_key, d_value = carried
        query_blk, seg_blk, pos_blk, total_blk, d_out = inputs
        scores = scores_of(query_blk, seg_blk, pos_blk)
        prob_f32 = jnp.exp(scores - total_blk[..., None])
        prob_bf16 = prob_f32.astype(jnp.bfloat16)
        d_probs = jnp.einsum("qhd,khd->hqk", d_out, values_all, preferred_element_type=jnp.float32)
        inner_sum = jnp.sum(prob_f32 * d_probs, axis=-1, keepdims=True)
        d_scores = (prob_f32 * (d_probs - inner_sum)).astype(jnp.bfloat16)
        d_query = (
            jnp.einsum("hqk,khd->qhd", d_scores, keys_all, preferred_element_type=jnp.float32)
            * score_scale
        )
        d_key = (
            d_key
            + jnp.einsum("hqk,qhd->khd", d_scores, query_blk, preferred_element_type=jnp.float32)
            * score_scale
        )
        d_value = d_value + jnp.einsum(
            "hqk,qhd->khd", prob_bf16, d_out, preferred_element_type=jnp.float32
        )
        return ((d_key, d_value), d_query)

    zero_keys = jnp.zeros((group_rows, local_heads, head_dim), jnp.float32)
    (d_key, d_value), d_query = lax.scan(
        backward_block,
        (zero_keys, zero_keys),
        (query_blocks, seg_blocks, pos_blocks, log_total, d_blocks),
    )
    owned_grads = lax.psum_scatter(
        jnp.stack([d_key, d_value], axis=1), "blk", scatter_dimension=0, tiled=True
    )
    grads_heads = jnp.concatenate(
        [d_query.reshape(shard_rows, 1, local_heads, head_dim), owned_grads], axis=1
    ).astype(jnp.bfloat16)
    cot_sums = jnp.sum(cotangent, axis=0, dtype=jnp.float32)
    d_linear = rotary_back(grads_heads.astype(jnp.float32))[0].reshape(shard_rows, 3 * col_width)
    d_linear_bf16 = d_linear.astype(jnp.bfloat16)
    d_one_terms = lax.dot_general(
        d_linear_bf16, qkv_cols, contract_last, preferred_element_type=jnp.float32
    )
    d_norm_one, d_norm_two = (
        lax.psum_scatter(d_one_terms, "head", scatter_dimension=0, tiled=True),
        lax.psum_scatter(d_two_terms, "head", scatter_dimension=0, tiled=True),
    )
    group_block = model_width // weight_owners
    block_sum = lax.psum_scatter(
        jnp.concatenate(
            [
                lax.dot_general(
                    attn_rows, d_linear_bf16, contract_rows, preferred_element_type=jnp.float32
                ),
                lax.dot_general(
                    attn_full, cot_cols, contract_rows, preferred_element_type=jnp.float32
                ),
                lax.dot_general(
                    mlp_rows, d_up_bf16, contract_rows, preferred_element_type=jnp.float32
                ),
                lax.dot_general(
                    cot_rows, act_bf16, contract_rows, preferred_element_type=jnp.float32
                ),
            ],
            axis=1,
        ),
        ("dp", "blk"),
        scatter_dimension=0,
        tiled=True,
    )
    part_qkv = block_sum[:, : 3 * col_width].reshape(group_block, 3, 1, col_width)
    part_out = block_sum[:, 3 * col_width : 4 * col_width].reshape(group_block, 1, 1, col_width)
    part_up = block_sum[:, 4 * col_width : 4 * col_width + ff_cols].reshape(
        group_block, 1, 1, ff_cols
    )
    part_down = block_sum[:, 4 * col_width + ff_cols :].reshape(group_block, 1, 1, ff_cols)
    owned_qkv, owned_out, owned_up, owned_down = (
        lax.all_to_all(part_qkv, "head", split_axis=0, concat_axis=2, tiled=True),
        lax.all_to_all(part_out, "head", split_axis=0, concat_axis=2, tiled=True),
        lax.all_to_all(part_up, "head", split_axis=0, concat_axis=2, tiled=True),
        lax.all_to_all(part_down, "head", split_axis=0, concat_axis=2, tiled=True),
    )
    grad_w_qkv = owned_qkv.reshape(owner_rows, 3 * model_width)
    grad_w_out = owned_out.reshape(owner_rows, model_width)
    grad_w_up = owned_up.reshape(owner_rows, hidden_units)
    grad_w_down = owned_down.reshape(owner_rows, hidden_units)
    selector = (jnp.arange(head_count, dtype=jnp.int32) == head_index).astype(jnp.float32)
    linear_sums = jnp.sum(d_linear_bf16, axis=0, dtype=jnp.float32).reshape(3, col_width)
    qkv_sums = (linear_sums[:, None, :] * selector[None, :, None]).reshape(3 * model_width)
    up_local = jnp.sum(d_up_bf16, axis=0, dtype=jnp.float32)
    up_sums = (up_local[None, :] * selector[:, None]).reshape(hidden_units)
    d_from_one, gain_one, shift_one = norm_back_one(d_norm_one)
    d_from_two, gain_two, shift_two = norm_back_two(d_norm_two)
    d_tokens = cot_f32 + d_from_one + d_from_two
    small_sums = lax.psum(
        (gain_one, shift_one, gain_two, shift_two, qkv_sums, cot_sums, up_sums),
        ("dp", "blk", "head"),
    )
    return (
        block_output,
        d_tokens,
        small_sums[0],
        small_sums[1],
        small_sums[2],
        small_sums[3],
        grad_w_qkv,
        small_sums[4],
        grad_w_out,
        small_sums[5],
        grad_w_up,
        small_sums[6],
        grad_w_down,
        small_sums[5],
    )


RUN = 256
TILE = 512
PLANE = ("blk", "head")
NT = (((1,), (1,)), ((), ()))
TN = (((0,), (0,)), ((), ()))


def turn(part, cosine, sine):
    lane = lax.broadcasted_iota(jnp.int32, part.shape, 1)
    half = ROT // 2
    other = jnp.where(lane < half, pltpu.roll(part, 128 - half, 1), pltpu.roll(part, half, 1))
    return part * cosine + other * sine


def fold_rows(value):
    return value.reshape(value.shape[0] // 8, 8, value.shape[1])


def attention_kernel(
    order_ref,
    lin_a,
    lin_b,
    cot_a,
    cot_b,
    cos_ref,
    sin_ref,
    out_ref,
    dlin_ref,
    sums_ref,
    q_c,
    k_c,
    v_c,
    d_c,
    kt_c,
    vt_c,
    dk_c,
    dv_c,
    s_c,
    p_c,
    ot_c,
):
    step = pl.program_id(0)
    prompt_tiles = (RUN * 8) // TILE
    f32 = jnp.float32
    bf16 = jnp.bfloat16

    @pl.when(step == 0)
    def _():
        sums_ref[...] = jnp.zeros_like(sums_ref)

    for side, (lin, cot) in enumerate(((lin_a, cot_a), (lin_b, cot_b))):
        run = step * 2 + side
        rows = pl.ds(pl.multiple_of(run * RUN, RUN), RUN)
        table = jnp.minimum(run, 8)
        cosine = cos_ref[table]
        sine = sin_ref[table]
        for part, target in ((0, q_c), (1, k_c)):
            base = part * HD
            turned = turn(lin[:, base : base + 128], cosine, sine)
            whole = jnp.concatenate([turned, lin[:, base + 128 : base + HD]], axis=1).astype(bf16)
            if part == 0:
                target[rows, :] = whole * jnp.asarray(HD**-0.5, bf16)
            else:
                target[rows, :] = whole
                kt_c[:, rows] = whole.T
        value = lin[:, 2 * HD :].astype(bf16)
        v_c[rows, :] = value
        vt_c[:, rows] = value.T
        d_c[rows, :] = cot[...]

    def rows_of(tile):
        return pl.ds(pl.multiple_of(tile * TILE, TILE), TILE)

    own = rows_of(step)
    query = q_c[own, :]
    d_out = d_c[own, :]
    before = jnp.minimum(step, prompt_tiles)

    def scores_of(tile):
        return lax.dot_general(k_c[rows_of(tile), :], query, NT, preferred_element_type=f32)

    def first(tile, top):
        scores = scores_of(tile)
        s_c[tile] = scores
        return jnp.maximum(top, jnp.max(fold_rows(scores), axis=0))

    key_row = lax.broadcasted_iota(jnp.int32, (TILE, TILE), 0)
    query_col = lax.broadcasted_iota(jnp.int32, (TILE, TILE), 1)
    same_run = (key_row // RUN) == (query_col // RUN)
    seen = (key_row <= query_col) & (same_run | (step < prompt_tiles))
    masked = jnp.where(seen, scores_of(step), -1e30)
    s_c[prompt_tiles] = masked
    top = lax.fori_loop(0, before, first, jnp.max(fold_rows(masked), axis=0))
    top = jnp.max(top, axis=0, keepdims=True)

    def second(slot, tile, carry):
        total, inner = carry
        grown = jnp.exp(s_c[slot] - top)
        s_c[slot] = grown
        d_prob = lax.dot_general(v_c[rows_of(tile), :], d_out, NT, preferred_element_type=f32)
        p_c[slot] = d_prob
        add = jnp.dot(vt_c[:, rows_of(tile)], grown.astype(bf16), preferred_element_type=f32)
        return (
            total + jnp.sum(fold_rows(grown), axis=0),
            inner + jnp.sum(fold_rows(grown * d_prob), axis=0),
            add,
        )

    zero = jnp.zeros((8, TILE), f32)
    total, inner, add = second(prompt_tiles, step, (zero, zero))
    ot_c[...] = add

    def second_loop(tile, carry):
        total, inner, add = second(tile, tile, carry)
        ot_c[...] += add
        return (total, inner)

    total, inner = lax.fori_loop(0, before, second_loop, (total, inner))
    scale = 1.0 / jnp.sum(total, axis=0, keepdims=True)
    inner = jnp.sum(inner, axis=0, keepdims=True) * scale
    attended = (ot_c[...] * scale).astype(bf16).T

    def third(slot, tile):
        prob = s_c[slot] * scale
        d_value = jnp.dot(prob.astype(bf16), d_out, preferred_element_type=f32)
        d_score = (prob * (p_c[slot] - inner)).astype(bf16)
        d_key = jnp.dot(d_score, query, preferred_element_type=f32)
        d_query = jnp.dot(kt_c[:, rows_of(tile)], d_score, preferred_element_type=f32)
        return d_value, d_key, d_query

    d_value, d_key, d_query = third(prompt_tiles, step)
    dv_c[own, :] = d_value
    dk_c[own, :] = d_key
    ot_c[...] = d_query

    def third_loop(tile, carry):
        d_value, d_key, d_query = third(tile, tile)
        dv_c[rows_of(tile), :] += d_value
        dk_c[rows_of(tile), :] += d_key
        ot_c[...] += d_query
        return carry

    lax.fori_loop(0, before, third_loop, 0)
    d_query = (ot_c[...] * HD**-0.5).T

    def put(run, part, grad):
        table = jnp.minimum(run, 8)
        turned = turn(grad[:, :128], cos_ref[table], -sin_ref[table])
        whole = jnp.concatenate([turned, grad[:, 128:]], axis=1) if part < 2 else grad
        whole = whole.astype(bf16)
        columns = slice(part * HD, part * HD + HD)
        dlin_ref[pl.ds(pl.multiple_of(order_ref[run] * RUN, RUN), RUN), columns] = whole
        sums_ref[:, columns] += jnp.sum(fold_rows(whole.astype(f32)), axis=0)

    for side in range(2):
        run = step * 2 + side
        piece = slice(side * RUN, side * RUN + RUN)
        put(run, 0, d_query[piece])
        out_ref[pl.ds(pl.multiple_of(order_ref[run] * RUN, RUN), RUN), :] = attended[piece]

    @pl.when(step == pl.num_programs(0) - 1)
    def _():
        def finish(run, carry):
            rows = pl.ds(pl.multiple_of(run * RUN, RUN), RUN)
            put(run, 1, dk_c[rows, :])
            put(run, 2, dv_c[rows, :])
            return carry

        lax.fori_loop(0, 2 * pl.num_programs(0), finish, 0)


def attention(order, linear, d_attn, cosine, sine):
    rows = linear.shape[0]
    bf16, f32 = jnp.bfloat16, jnp.float32
    whole = lambda shape: pl.BlockSpec(
        shape, lambda i, o: (0,) * len(shape), pipeline_mode=pl.Buffered(1)
    )
    run_of = lambda side, width: pl.BlockSpec((RUN, width), lambda i, o: (o[2 * i + side], 0))
    slots = (RUN * 8) // TILE + 1
    return pl.pallas_call(
        attention_kernel,
        out_shape=(
            jax.ShapeDtypeStruct((rows, HD), bf16),
            jax.ShapeDtypeStruct((rows, 3 * HD), bf16),
            jax.ShapeDtypeStruct((8, 3 * HD), f32),
        ),
        grid_spec=pltpu.PrefetchScalarGridSpec(
            num_scalar_prefetch=1,
            grid=(rows // TILE,),
            in_specs=[
                run_of(0, 3 * HD),
                run_of(1, 3 * HD),
                run_of(0, HD),
                run_of(1, HD),
                whole(cosine.shape),
                whole(sine.shape),
            ],
            out_specs=[whole((rows, HD)), whole((rows, 3 * HD)), whole((8, 3 * HD))],
            scratch_shapes=[pltpu.VMEM((rows, HD), bf16)] * 4
            + [pltpu.VMEM((HD, rows), bf16)] * 2
            + [pltpu.VMEM((rows, HD), f32)] * 2
            + [pltpu.VMEM((slots, TILE, TILE), f32)] * 2
            + [pltpu.VMEM((HD, TILE), f32)],
        ),
        compiler_params=pltpu.CompilerParams(
            dimension_semantics=("arbitrary",), vmem_limit_bytes=60 << 20
        ),
        cost_estimate=pl.CostEstimate(
            flops=24_000_000_000, transcendentals=8_000_000, bytes_accessed=24_000_000
        ),
    )(order, linear, linear, d_attn, d_attn, cosine, sine)


def swap(value, bits):
    plane = lax.axis_size(PLANE)
    return lax.ppermute(value, PLANE, [(p, p ^ bits) for p in range(plane)])


def norm_kernel(x_ref, scale_ref, *refs):
    attn_ref, mlp_ref = refs[-2:]
    value = x_ref[...].astype(jnp.float32)
    centered = value - jnp.mean(value, axis=-1, keepdims=True)
    variance = jnp.mean(centered * centered, axis=-1, keepdims=True)
    normed = centered * lax.rsqrt(variance + 1e-05)
    attn_ref[...] = (normed * scale_ref[0:1, :] + scale_ref[1:2, :]).astype(jnp.bfloat16)
    mlp_ref[...] = (normed * scale_ref[2:3, :] + scale_ref[3:4, :]).astype(jnp.bfloat16)


def norm_into(block, scales, filled, first, total):
    count, width = block.shape
    step = 128
    spec = pl.BlockSpec((step, width), lambda i: (first // step + i, 0))
    shape = jax.ShapeDtypeStruct((total, width), jnp.bfloat16)
    kept = pl.BlockSpec(memory_space=pl.ANY)
    return pl.pallas_call(
        norm_kernel,
        out_shape=(shape, shape),
        grid=(count // step,),
        in_specs=[
            pl.BlockSpec((step, width), lambda i: (i, 0)),
            pl.BlockSpec(scales.shape, lambda i: (0, 0)),
        ]
        + [kept] * len(filled),
        out_specs=(spec, spec),
        input_output_aliases={2: 0, 3: 1} if filled else {},
        cost_estimate=pl.CostEstimate(
            flops=12 * count * width, transcendentals=count, bytes_accessed=6 * count * width
        ),
    )(block, scales, *filled)


def after(value, *others):
    return lax.optimization_barrier((value, *others))[0]


def total_of(value, axis_bits, axes):
    for bits in axis_bits:
        count = lax.axis_size(axes)
        value = value + lax.ppermute(value, axes, [(p, p ^ bits) for p in range(count)])
    return value


def shards_by_heads(
    tokens,
    cotangent,
    segment,
    position,
    ln1_gain,
    ln1_bias,
    ln2_gain,
    ln2_bias,
    w_qkv,
    b_qkv,
    w_out,
    b_out,
    w_up,
    b_up,
    w_down,
    b_down,
):
    bf16, f32 = jnp.bfloat16, jnp.float32
    rows, width = tokens.shape
    hidden = w_up.shape[1]
    planes = lax.axis_size("dp")
    plane = lax.axis_size(PLANE)
    p_at = lax.axis_index(PLANE)
    owned = w_qkv.shape[0]
    slice_ff = hidden // plane

    marks = jnp.stack([segment[::RUN], position[::RUN]], axis=1)
    marks = jnp.pad(marks, ((0, 8 - marks.shape[0]), (0, 126)))

    def to_columns(weight):
        sent = lax.all_to_all(weight.transpose(1, 0, 2), PLANE, split_axis=0, concat_axis=0, tiled=True)
        return sent.reshape(plane * owned, weight.shape[2])

    half = rows // 2
    total = plane * rows
    scales = jnp.pad(jnp.stack([ln1_gain, ln1_bias, ln2_gain, ln2_bias]), ((0, 4), (0, 0)))
    up_cols = to_columns(w_up.reshape(owned, plane, slice_ff))
    tok_x, tok_y = swap(tokens, 4), swap(tokens, 1)
    tok_c = swap(tokens, 2)
    qkv_own = w_qkv.reshape(owned, 3, plane, HD).transpose(0, 2, 1, 3).reshape(owned, plane, 3 * HD)
    qkv_cols = to_columns(after(qkv_own, up_cols))
    down_cols = to_columns(after(w_down.reshape(owned, plane, slice_ff), qkv_cols))
    inputs = norm_into(tokens, scales, (), 0, total)
    inputs = norm_into(tok_c, scales, inputs, 4 * rows, total)
    tok_far, tok_far_too = swap(tok_y[:half], 4), swap(tok_x[half:], 1)
    for piece, place in ((tok_x, rows), (tok_y, 2 * rows)):
        inputs = norm_into(piece, scales, inputs, place, total)
        inputs = norm_into(swap(piece, 2), scales, inputs, place + 4 * rows, total)
    for piece, place in ((tok_far, 3 * rows), (tok_far_too, 3 * rows + half)):
        inputs = norm_into(piece, scales, inputs, place, total)
        inputs = norm_into(swap(piece, 2), scales, inputs, place + 4 * rows, total)
    a_all, m_all = inputs
    cot_sent = after(cotangent, tok_far, tok_far_too)
    cot_x, cot_y = swap(cot_sent, 4), swap(cot_sent, 1)
    cot_sums = jnp.sum(cot_sent, axis=0, dtype=f32)

    w_ff = lax.all_gather(up_cols, "dp", axis=0, tiled=True)
    head_out = jnp.concatenate([qkv_cols, w_out.reshape(plane * owned, width // plane)], axis=1)
    head_out = lax.all_gather(head_out, "dp", axis=0, tiled=True)
    w_dn = lax.all_gather(down_cols, "dp", axis=0, tiled=True)
    w_head = head_out[:, : 3 * HD]
    out_rows = head_out[:, 3 * HD :].reshape(planes, owned, width)

    parts = HD // owned
    per_plane = HEADS // planes

    def to_head(turn_at):
        return [(p, per_plane * ((p % parts - turn_at) % parts) + p // parts) for p in range(plane)]

    w_o = jnp.zeros((parts, owned, width), bf16)
    for turn_at in range(parts):
        piece = lax.dynamic_index_in_dim(out_rows, (p_at % parts - turn_at) % parts, 0, keepdims=False)
        got = lax.ppermute(piece, PLANE, to_head(turn_at))
        w_o = lax.dynamic_update_index_in_dim(w_o, got, (turn_at + p_at // per_plane) % parts, 0)
    w_o = w_o.reshape(HD, width)
    lane = lax.broadcasted_iota(jnp.int32, (9 * RUN, 128), 1)
    place = lax.broadcasted_iota(jnp.int32, (9 * RUN, 128), 0).astype(f32)
    pairs = ROT // 2
    frequency = jnp.exp((lane % pairs).astype(f32) * (-2.0 * math.log(10000.0) / ROT))
    angle = place * frequency
    cosine = jnp.where(lane < ROT, jnp.cos(angle), 1.0).reshape(9, RUN, 128)
    sine = jnp.where(lane < pairs, -jnp.sin(angle), jnp.sin(angle))
    sine = jnp.where(lane < ROT, sine, 0.0).reshape(9, RUN, 128)

    w_ff = after(w_ff, cosine, sine)
    b_ff = lax.dynamic_slice_in_dim(b_up, p_at * slice_ff, slice_ff)
    up_linear = jnp.dot(m_all, w_ff, preferred_element_type=f32) + b_ff
    below = 0.5 + 0.5 * lax.erf(up_linear * (0.5**0.5))
    act = (up_linear * below).astype(bf16)
    slope = below + up_linear * jnp.exp(-0.5 * up_linear * up_linear) * ((2.0 * math.pi) ** -0.5)
    act, slope = lax.optimization_barrier((act, slope.astype(bf16)))

    cot_own, cot_x, cot_y = lax.optimization_barrier((cot_sent, cot_x, cot_y, act))[:3]
    cot_far, cot_far_too = swap(cot_y[:half], 4), swap(cot_x[half:], 1)
    near = [cot_own, cot_x, cot_y, cot_far, cot_far_too]
    cot_all = jnp.concatenate(near + [swap(piece, 2) for piece in near], axis=0)
    marks = swap_marks(after(marks, cot_far, cot_far_too))
    seg_run, pos_run = marks[:, 0], marks[:, 1]
    rank = jnp.where(seg_run == 0, pos_run // RUN, seg_run + 7)
    order = jnp.argsort(rank).astype(jnp.int32)

    def summed(grad):
        return lax.psum_scatter(grad, "dp", scatter_dimension=0, tiled=True)

    def owner_rows(grad):
        back = lax.all_to_all(grad.reshape(plane, owned, -1), PLANE, split_axis=0, concat_axis=0, tiled=True)
        return back.astype(f32)

    def grad_of(left, right):
        return lax.dot_general(left, right, TN, preferred_element_type=f32)

    def plane_sum(terms):
        def plus(late, first, last, *added):
            value = terms(late, first, last)
            for more in added:
                value = value + more.astype(f32)
            return value.astype(bf16)

        def start(*late):
            mine = plus(late, 4 * rows, 8 * rows)
            return mine, swap(mine, 2)

        def far(other, *late):
            mine = plus(late, 3 * rows, 4 * rows, other[3 * rows :])
            return mine, swap(mine[:half], 4), swap(mine[half:], 1)

        def sides(other, far_y, far_x, *late):
            far_x = jnp.pad(far_x, ((half, 0), (0, 0)))
            far_y = jnp.pad(far_y, ((0, half), (0, 0)))
            to_x = plus(late, rows, 2 * rows, other[rows : 2 * rows], far_x)
            to_y = plus(late, 2 * rows, 3 * rows, other[2 * rows : 3 * rows], far_y)
            return to_x, to_y, swap(to_x, 4), swap(to_y, 1)

        def finish(other, got_x, got_y, *late):
            value = terms(late, 0, rows) + other[:rows].astype(f32)
            return value + got_x.astype(f32) + got_y.astype(f32)

        return start, far, sides, finish

    b_head = lax.dynamic_index_in_dim(b_qkv.reshape(3, plane, HD), p_at, 1, keepdims=False)
    linear = jnp.dot(a_all, after(w_head, act), preferred_element_type=f32) + b_head.reshape(3 * HD)
    g_down = grad_of(cot_all, after(act, linear)).astype(bf16)
    d_attn = lax.dot_general(cot_all, after(w_o, g_down), NT, preferred_element_type=f32).astype(bf16)
    attn, d_linear, head_sums = attention(order, linear, d_attn, cosine, sine)
    g_down = summed(g_down)

    z_head = grad_of(a_all, d_linear)
    z_low = z_head.astype(bf16)
    g_out = grad_of(attn, cot_all).astype(bf16).reshape(parts, owned, width)
    out_parts = jnp.zeros((parts, owned, width), bf16)
    for turn_at in range(parts):
        piece = lax.dynamic_index_in_dim(g_out, (turn_at + p_at // per_plane) % parts, 0, keepdims=False)
        got = lax.ppermute(piece, PLANE, [(b, a) for a, b in to_head(turn_at)])
        out_parts = lax.dynamic_update_index_in_dim(out_parts, got, (p_at % parts - turn_at) % parts, 0)
    head_sum = jnp.concatenate([z_low, out_parts.reshape(width, HD)], axis=1)
    head_sum = summed(head_sum)

    branch_in = jnp.concatenate([attn, act], axis=1)
    branch_w = jnp.concatenate([w_o, w_dn.T], axis=0)
    b_start, b_far, b_sides, b_finish = plane_sum(
        lambda late, i, j: jnp.dot(after(branch_in, *late)[i:j], branch_w, preferred_element_type=f32),
    )
    b_terms, b_other = b_start(g_out, z_low)

    d_act = jnp.dot(cot_all, after(w_dn, b_terms), preferred_element_type=f32)
    d_up = (d_act * slope.astype(f32)).astype(bf16)
    far_terms, far_y, far_x = b_far(b_other, d_up)

    d_in = jnp.concatenate([d_linear, d_up], axis=1)
    d_w = jnp.concatenate(
        [
            (w_head.astype(f32) * ln1_gain[:, None]).astype(bf16),
            (w_ff.astype(f32) * ln2_gain[:, None]).astype(bf16),
        ],
        axis=1,
    )
    p_start, p_far, p_sides, p_finish = plane_sum(
        lambda late, i, j: lax.dot_general(
            after(d_in, *late)[i:j], d_w, NT, preferred_element_type=f32
        ),
    )
    p_terms, p_other = p_start(far_terms)
    to_x, to_y, b_x, b_y = b_sides(b_other, far_y, far_x, p_terms)
    far_terms, far_y, far_x = p_far(p_other, to_x, to_y)
    z_up = lax.optimization_barrier(grad_of(m_all, after(d_up, far_terms)).astype(bf16))
    z_up_sum = summed(z_up)
    to_x, to_y, p_x, p_y = p_sides(p_other, far_y, far_x, z_up)
    branch = b_finish(b_other, b_x, b_y, to_x, to_y)
    block_output = (tokens.astype(f32) + branch + (b_out + b_down)).astype(bf16)
    pulled = p_finish(p_other, p_x, p_y, block_output)
    tokens_f32 = tokens.astype(f32)
    centered = tokens_f32 - jnp.mean(tokens_f32, axis=-1, keepdims=True)
    spread = lax.rsqrt(jnp.mean(centered * centered, axis=-1, keepdims=True) + 1e-05)
    normed = centered * spread
    d_tokens = cotangent.astype(f32) + spread * (
        pulled
        - jnp.mean(pulled, axis=-1, keepdims=True)
        - normed * jnp.mean(pulled * normed, axis=-1, keepdims=True)
    )

    head_sums = jnp.sum(head_sums, axis=0)
    ff_sums = jnp.sum(d_up, axis=0, dtype=f32)
    shift_head = jnp.sum(w_head.astype(f32) * head_sums, axis=1)
    shift_ff = jnp.sum(w_ff.astype(f32) * ff_sums, axis=1)
    gain_head = (jnp.sum(z_head * w_head.astype(f32), axis=1) - ln1_bias * shift_head) / ln1_gain
    gain_ff = (jnp.sum(z_up.astype(f32) * w_ff.astype(f32), axis=1) - ln2_bias * shift_ff) / ln2_gain
    gain_head = after(gain_head, to_x, to_y, block_output)
    small = jnp.concatenate([gain_head, shift_head, gain_ff, shift_ff, cot_sums]).reshape(-1, 128)
    sums = jnp.concatenate([head_sums, ff_sums]).reshape(-1, 128)
    count = sums.shape[0]
    both = total_of(jnp.concatenate([sums, small], axis=0), (1, 2), "dp")
    sums, small = both[:count], both[count:]
    sums = lax.dynamic_update_slice_in_dim(jnp.zeros((plane * count, 128), f32), sums, p_at * count, 0)
    both = total_of(jnp.concatenate([sums, small], axis=0), (1, 4, 2), PLANE)
    sums, small = both[: plane * count].reshape(plane, count * 128), both[plane * count :].reshape(5, width)
    grad_b_qkv = sums[:, : 3 * HD].reshape(plane, 3, HD).transpose(1, 0, 2).reshape(3 * width)
    grad_b_up = sums[:, 3 * HD :].reshape(hidden)

    z_qkv = owner_rows(head_sum[:, : 3 * HD]).reshape(plane, owned, 3, HD).transpose(1, 2, 0, 3)
    grad_w_qkv = z_qkv.reshape(owned, 3 * width)
    grad_w_up = owner_rows(z_up_sum).transpose(1, 0, 2).reshape(owned, hidden)
    grad_w_down = owner_rows(g_down).transpose(1, 0, 2).reshape(owned, hidden)
    grad_w_out = head_sum[:, 3 * HD :].reshape(owned, width).astype(f32)
    return (
        block_output,
        d_tokens,
        small[0],
        small[1],
        small[2],
        small[3],
        grad_w_qkv,
        grad_b_qkv,
        grad_w_out,
        small[4],
        grad_w_up,
        grad_b_up,
        grad_w_down,
        small[4],
    )


def swap_marks(marks):
    mine = marks[:2]
    got = swap(marks, 4)[:2]
    pair = jnp.concatenate([mine, got], axis=0)
    pair = jnp.pad(pair, ((0, 4), (0, 0)))
    four = jnp.concatenate([pair[:4], swap(pair, 1)[:4]], axis=0)
    return jnp.concatenate([four, swap(four, 2)], axis=0)


def layer(*arrays):
    return shards_by_heads(*arrays)


def solution(mesh):
    plane = mesh.shape["blk"] * mesh.shape["head"]
    by_heads = plane == HEADS
    body = layer if by_heads else shards_by_blocks
    placed = (
        P(("dp", "blk", "head"), None),
        P(("dp", "blk", "head"), None),
        P(("dp", "blk", "head")),
        P(("dp", "blk", "head")),
        P(),
        P(),
        P(),
        P(),
        P(("dp", "blk", "head"), None),
        P(),
        P(("dp", "blk", "head"), None),
        P(),
        P(("dp", "blk", "head"), None),
        P(),
        P(("dp", "blk", "head"), None),
        P(),
    )
    return jax.shard_map(
        body,
        mesh=mesh,
        in_specs=placed,
        out_specs=(
            P(("dp", "blk", "head"), None),
            P(("dp", "blk", "head"), None),
            P(),
            P(),
            P(),
            P(),
            P(("dp", "blk", "head"), None),
            P(),
            P(("dp", "blk", "head"), None),
            P(),
            P(("dp", "blk", "head"), None),
            P(),
            P(("dp", "blk", "head"), None),
            P(),
        ),
        check_vma=False,
    )
```
